32 devices in a mesh: copy: 4 (over x, core), fsdp: 8 (over z, y).
Axes of the slice: x: 2, y: 2, z: 4, core: 2. Of those that a mesh axis runs over, the one named last changes fastest.
Arguments:
- student_hidden: bfloat16 [4, 32, 96, 1024], P('copy', 'fsdp'), may hold values from -6 to 6
- keep_index: int32 [4, 32, 96], P(None, 'fsdp'), may hold values from 0 to 191, as said below
- lengths: int32 [32], P('fsdp'), may hold values from 48 to 192
- teacher_layers: bfloat16 [4, 4, 8, 192, 1024], P(None, 'copy', 'fsdp')
- w_in: bfloat16 [1024, 2048], P('fsdp'), may hold values from -0.1875 to 0.1875
- w_out: bfloat16 [2048, 1024], P('fsdp'), may hold values from -0.125 to 0.125
- dec_in: bfloat16 [1024, 384], P('fsdp'), may hold values from -0.1875 to 0.1875
- dec_conv: bfloat16 [384, 2, 7, 384], P('fsdp'), may hold values from -0.125 to 0.125
- dec_out: bfloat16 [384, 1024], P('fsdp'), may hold values from -0.3125 to 0.3125
Outputs:
- loss: float32 [], replicated
- grad_hidden: bfloat16 [4, 32, 96, 1024], P('copy', 'fsdp')
- grad_w_in: bfloat16 [1024, 2048], P('fsdp')
- grad_w_out: bfloat16 [2048, 1024], P('fsdp')
- grad_dec_in: bfloat16 [1024, 384], P('fsdp')
- grad_dec_conv: bfloat16 [384, 2, 7, 384], P('fsdp')
- grad_dec_out: bfloat16 [384, 1024], P('fsdp')
The draws below stay inside these ranges and needn't reach their ends.
Inputs may be any that keep to these rules, and one draw needn't show every extreme that they name: Each row keep_index[c, u, :] holds 96 distinct frame positions in rising order.
All inputs are finite; a program needn't handle non-finite values.
Results may differ from the reference program's by a relative error of at most 0.024.
Values may be sent and summed in bfloat16 or wider, within the bound.
A program may use at most 128 MiB of HBM per device.

```python
import math
import jax
import jax.numpy as jnp
from jax import lax

D = 1024
FF = 2048
CD = 384
KW = 7
DEC_LAYERS = 2
TOPK = 4
UTT_DEV = 4
FRAMES = 192
KEEP = 96
MASKED = 96
COPIES = 4
UTTS = 32
N_COPY = 4
N_FSDP = 8


def draw_keep_index(key, part):
    noise = jax.random.randint(key, (COPIES, UTTS, FRAMES), 0, FRAMES)
    position = jnp.arange(FRAMES, dtype=jnp.int32)[None, None, :]
    lean = (2 * jnp.arange(COPIES, dtype=jnp.int32) - (COPIES - 1))[:, None, None]
    score = (noise + lean * position // 2) * FRAMES + position
    order = jnp.argsort(-score, axis=-1, stable=True)[:, :, :KEEP]
    return jnp.sort(order, axis=-1).astype(jnp.int32)


def draw_lengths(key, part):
    key_jitter, key_long = jax.random.split(key, 2)
    position = jnp.arange(UTTS, dtype=jnp.int32)
    groups = UTTS // UTT_DEV
    rank = position // UTT_DEV
    base = FRAMES // 4 + 3 * FRAMES // 4 * rank // max(groups - 1, 1)
    jitter = jax.random.randint(key_jitter, (UTTS,), 0, FRAMES // 8 + 1)
    spread = jnp.clip(base + jitter - FRAMES // 16, FRAMES // 4, FRAMES)
    longest = jax.random.randint(key_long, (), 0, UTTS)
    return jnp.where(position == longest, FRAMES, spread).astype(jnp.int32)


def draw_teacher_layers(key, part):
    key_noise, key_frame, key_scale, key_mean = jax.random.split(key, 4)
    shape = (TOPK, COPIES, UTTS // COPIES, FRAMES, D)
    noise = jax.random.normal(key_noise, shape, jnp.float32)
    frame_scale = jnp.exp(jax.random.uniform(key_frame, (TOPK, COPIES, UTTS // COPIES, FRAMES, 1), jnp.float32, math.log(0.3), math.log(3.0)))
    channel_scale = jnp.exp(jax.random.uniform(key_scale, (TOPK, COPIES, UTTS // COPIES, 1, D), jnp.float32, math.log(0.3), math.log(3.0)))
    channel_mean = jax.random.normal(key_mean, (TOPK, COPIES, UTTS // COPIES, 1, D), jnp.float32) * 1.5
    return (channel_mean + channel_scale * frame_scale * noise).astype(jnp.bfloat16)


def with_spikes(values, stream_key, source, target, parts, factor):
    owner, partner = [(jnp.arange(values.shape[axis_at]) // (values.shape[axis_at] // parts)).reshape([-1 if axis == axis_at else 1 for axis in range(values.ndim)]) for axis_at in (source, target)]
    chosen = jax.random.permutation(stream_key, parts)[partner]
    strong = (owner == chosen) | (owner == (partner + parts // 2) % parts)
    return jnp.where(strong, factor * values, values)


def shard_levels(own_key, extent, pieces, low, top_value):
    def one(axis_at, parts):
        steps = jax.random.uniform(jax.random.fold_in(jax.random.fold_in(own_key, 6), axis_at), (parts,), jnp.float32, low / len(pieces), top_value / len(pieces))
        return jnp.repeat(jnp.exp(steps), extent[axis_at] // parts).reshape((-1,) + (1,) * (len(extent) - axis_at - 1))

    gain = one(*pieces[0])
    for cut in pieces[1:]:
        gain = gain * one(*cut)
    return gain


def bell_draw(rng, extent, scale, limit, cuts=(), held_as=jnp.bfloat16):
    entries = scale * jax.random.normal(rng, extent, jnp.float32)
    if cuts:
        entries = entries * shard_levels(rng, extent, cuts, -0.22, 0.18)
    return jnp.clip(entries, -limit, limit).astype(held_as)


def gaussian_with(own_key, extent, scale, most, cuts, heavy, kind=jnp.bfloat16):
    drawn = scale * jax.random.normal(own_key, extent, jnp.float32)
    if cuts:
        drawn = drawn * shard_levels(own_key, extent, cuts, -0.22, 0.18)
    return jnp.clip(with_spikes(drawn, jax.random.fold_in(own_key, 3), *heavy), -most, most).astype(kind)


def setup_inputs(seed: int = 0) -> dict:
    arg_keys = jax.random.split(jax.random.key(seed), 10)
    return {
        "student_hidden": gaussian_with(arg_keys[0], (COPIES, UTTS, KEEP, D), 1.0, 6.0, ((0, 4), (1, 8)), (1, 3, 8, 2.0)),
        "keep_index": draw_keep_index(jax.random.fold_in(arg_keys[9], 71), 0),
        "lengths": draw_lengths(jax.random.fold_in(arg_keys[9], 71), 0),
        "teacher_layers": draw_teacher_layers(jax.random.fold_in(arg_keys[9], 71), 0),
        "w_in": bell_draw(arg_keys[4], (D, FF), D ** -0.5, 0.1875, ((0, 8),)),
        "w_out": bell_draw(arg_keys[5], (FF, D), FF ** -0.5, 0.125, ((0, 8),)),
        "dec_in": bell_draw(arg_keys[6], (D, CD), D ** -0.5, 0.1875, ((0, 8),)),
        "dec_conv": bell_draw(arg_keys[7], (CD, DEC_LAYERS, KW, CD), (KW * CD) ** -0.5, 0.125, ((0, 8),)),
        "dec_out": bell_draw(arg_keys[8], (CD, D), CD ** -0.5, 0.3125, ((0, 8),)),
    }


EPSILON = 1e-05
HALF_ROOT = 0.7071067811865476
GAUSS_PEAK = 0.3989422804014327

def layer_norm(values):
    center = values - lax.optimization_barrier(jnp.mean(values, axis=-1, keepdims=True))
    inv_scale = lax.rsqrt(lax.optimization_barrier(jnp.mean(center * center, axis=-1, keepdims=True)) + EPSILON)
    return (center * inv_scale, inv_scale)

def norm_backward(grad, normed, inv_scale):
    return inv_scale * (grad - lax.optimization_barrier(jnp.mean(grad, axis=-1, keepdims=True)) - normed * lax.optimization_barrier(jnp.mean(grad * normed, axis=-1, keepdims=True)))

def gelu_value(values):
    return 0.5 * values * (1.0 + lax.erf(values * HALF_ROOT))

def gelu_slope(values):
    return 0.5 * (1.0 + lax.erf(values * HALF_ROOT)) + values * jnp.exp(-0.5 * values * values) * GAUSS_PEAK

def unfold_frames(state, width):
    half = width // 2
    frames = state.shape[1]
    padded = jnp.pad(state, ((0, 0), (half, half), (0, 0)))
    return jnp.concatenate([padded[:, k:k + frames] for k in range(width)], axis=-1)

def fold_frames(grad, width, channels):
    units, frames = (grad.shape[0], grad.shape[1])
    half = width // 2
    split_grad = grad.reshape(units, frames, width, channels)
    padded = jnp.pad(split_grad, ((0, 0), (half, half), (0, 0), (0, 0)))
    total = jnp.zeros((units, frames, channels), grad.dtype)
    for k in range(width):
        total = total + padded[:, 2 * half - k:2 * half - k + frames, k]
    return total

def kernel_matrix(kernels, layer):
    return jnp.transpose(kernels[:, layer], (1, 0, 2)).reshape(-1, kernels.shape[3])

def teacher_targets(layer_outputs, lengths):
    frames = layer_outputs.shape[2]
    valid = (jnp.arange(frames, dtype=jnp.int32)[None, :] < lengths[:, None]).astype(jnp.float32)
    weight = valid[:, :, None]
    count = lax.optimization_barrier(jnp.sum(valid, axis=1))[:, None, None]
    total = jnp.zeros(layer_outputs.shape[1:], jnp.float32)
    for k in range(layer_outputs.shape[0]):
        values = layer_outputs[k].astype(jnp.float32)
        mean = lax.optimization_barrier(jnp.sum(values * weight, axis=1, keepdims=True)) / count
        center = values - mean
        variance = lax.optimization_barrier(jnp.sum(center * center * weight, axis=1, keepdims=True)) / count
        total = total + center * lax.rsqrt(variance + EPSILON)
    return (total * weight / layer_outputs.shape[0]).astype(jnp.bfloat16)

def block_step(hidden, keep, lens, targets, w_in, w_out, dec_in, dec_conv, dec_out):
    units, keep_count, width = hidden.shape
    frames = targets.shape[1]
    layers = dec_conv.shape[1]
    kernel = dec_conv.shape[2]
    channels = dec_conv.shape[3]
    rows = units * keep_count
    frame_index = jnp.arange(frames, dtype=jnp.int32)
    kept = jnp.any(keep[:, :, None] == frame_index[None, None, :], axis=1)
    valid = frame_index[None, :] < lens[:, None]
    masked = jnp.logical_and(valid, jnp.logical_not(kept)).astype(jnp.float32)
    hidden_rows = hidden.reshape(rows, width).astype(jnp.float32)
    normed_exact, inv_scale = layer_norm(hidden_rows)
    normed = normed_exact.astype(jnp.bfloat16)
    projected = jnp.dot(normed, w_in, preferred_element_type=jnp.float32)
    activation = gelu_value(projected).astype(jnp.bfloat16)
    student_out = (hidden_rows + jnp.dot(activation, w_out, preferred_element_type=jnp.float32)).astype(jnp.bfloat16)
    lifted = jnp.dot(student_out, dec_in, preferred_element_type=jnp.float32).astype(jnp.bfloat16)
    unit_index = jnp.arange(units, dtype=jnp.int32)[:, None]
    state = jnp.zeros((units, frames, channels), jnp.bfloat16).at[unit_index, keep].set(lifted.reshape(units, keep_count, channels))
    saved = []
    for layer in range(layers):
        unfolded = unfold_frames(state, kernel).reshape(units * frames, kernel * channels)
        convolved = jnp.dot(unfolded, kernel_matrix(dec_conv, layer), preferred_element_type=jnp.float32)
        conv_normed, conv_scale = layer_norm(convolved)
        result = gelu_value(conv_normed)
        if layer > 0:
            result = result + state.reshape(units * frames, channels).astype(jnp.float32)
        saved.append((unfolded, conv_normed, conv_scale))
        state = result.reshape(units, frames, channels).astype(jnp.bfloat16)
    final_state = state.reshape(units * frames, channels)
    prediction = jnp.dot(final_state, dec_out, preferred_element_type=jnp.float32)
    loss_scale = 1.0 / math.sqrt(width)
    error = (prediction - targets.reshape(units * frames, width).astype(jnp.float32)) * masked.reshape(units * frames, 1)
    total = jnp.sum(error * error) * loss_scale
    prediction_grad = (2.0 * loss_scale * error).astype(jnp.bfloat16)
    out_term = jnp.dot(final_state.T, prediction_grad, preferred_element_type=jnp.float32)
    state_grad = jnp.dot(prediction_grad, dec_out.T, preferred_element_type=jnp.float32)
    kernel_terms = [None] * layers
    for layer in reversed(range(layers)):
        unfolded, conv_normed, conv_scale = saved[layer]
        filter_grad = norm_backward(state_grad * gelu_slope(conv_normed), conv_normed, conv_scale).astype(jnp.bfloat16)
        kernel_terms[layer] = jnp.dot(unfolded.T, filter_grad, preferred_element_type=jnp.float32)
        unfold_grad = jnp.dot(filter_grad, kernel_matrix(dec_conv, layer).T, preferred_element_type=jnp.float32)
        previous_grad = fold_frames(unfold_grad.reshape(units, frames, kernel * channels), kernel, channels).reshape(units * frames, channels)
        if layer > 0:
            previous_grad = previous_grad + state_grad
        state_grad = previous_grad
    conv_term = jnp.stack([jnp.transpose(term.reshape(kernel, channels, channels), (1, 0, 2)) for term in kernel_terms], axis=1)
    lifted_grad = jnp.take_along_axis(state_grad.reshape(units, frames, channels), keep[:, :, None], axis=1).reshape(rows, channels).astype(jnp.bfloat16)
    in_term = jnp.dot(student_out.T, lifted_grad, preferred_element_type=jnp.float32)
    output_grad = jnp.dot(lifted_grad, dec_in.T, preferred_element_type=jnp.float32)
    output_half = output_grad.astype(jnp.bfloat16)
    out_proj_term = jnp.dot(activation.T, output_half, preferred_element_type=jnp.float32)
    activation_grad = jnp.dot(output_half, w_out.T, preferred_element_type=jnp.float32)
    projected_grad = (activation_grad * gelu_slope(projected)).astype(jnp.bfloat16)
    in_proj_term = jnp.dot(normed.T, projected_grad, preferred_element_type=jnp.float32)
    normed_grad = jnp.dot(projected_grad, w_in.T, preferred_element_type=jnp.float32)
    grad_hidden = (output_grad + norm_backward(normed_grad, normed_exact, inv_scale)).astype(jnp.bfloat16)
    terms = (in_proj_term, out_proj_term, in_term, conv_term, out_term)
    return (total, grad_hidden.reshape(units, keep_count, width), terms)

def reference(student_hidden, keep_index, lengths, teacher_layers, w_in, w_out, dec_in, dec_conv, dec_out):
    per_copy = UTT_DEV // N_COPY
    arranged = teacher_layers.reshape(TOPK, N_COPY, N_FSDP, per_copy, FRAMES, D)
    arranged = jnp.transpose(arranged, (0, 2, 1, 3, 4, 5)).reshape(TOPK, UTTS, FRAMES, D)
    targets = teacher_targets(arranged, lengths)
    blocks = N_COPY * N_FSDP
    zero_terms = (jnp.zeros((D, FF), jnp.float32), jnp.zeros((FF, D), jnp.float32), jnp.zeros((D, CD), jnp.float32), jnp.zeros((CD, DEC_LAYERS, KW, CD), jnp.float32), jnp.zeros((CD, D), jnp.float32))

    def scan_step(carry, block):
        sums, total = carry
        copy_index = block // N_FSDP
        start = (block % N_FSDP * UTT_DEV).astype(jnp.int32)
        hidden = lax.dynamic_slice_in_dim(lax.dynamic_index_in_dim(student_hidden, copy_index, 0, keepdims=False), start, UTT_DEV, 0)
        keep = lax.dynamic_slice_in_dim(lax.dynamic_index_in_dim(keep_index, copy_index, 0, keepdims=False), start, UTT_DEV, 0)
        lens = lax.dynamic_slice_in_dim(lengths, start, UTT_DEV, 0)
        block_targets = lax.dynamic_slice_in_dim(targets, start, UTT_DEV, 0)
        part_total, grad_hidden, terms = block_step(hidden, keep, lens, block_targets, w_in, w_out, dec_in, dec_conv, dec_out)
        sums = tuple((acc + lax.optimization_barrier(term.astype(jnp.bfloat16)).astype(jnp.float32) for acc, term in zip(sums, terms)))
        return ((sums, total + part_total), grad_hidden)
    start_carry = (zero_terms, jnp.zeros((), jnp.float32))
    (sums, total), hidden_grads = lax.scan(scan_step, start_carry, jnp.arange(blocks, dtype=jnp.int32))
    loss = total / float(N_COPY * UTTS * MASKED)
    grad_hidden = hidden_grads.reshape(N_COPY, UTTS, KEEP, D)
    return (loss, grad_hidden, sums[0].astype(jnp.bfloat16), sums[1].astype(jnp.bfloat16), sums[2].astype(jnp.bfloat16), sums[3].astype(jnp.bfloat16), sums[4].astype(jnp.bfloat16))
```

```python
import math

import jax
import jax.numpy as jnp
from jax import lax
from jax.experimental import pallas as pl
from jax.experimental.pallas import tpu as pltpu
from jax.sharding import PartitionSpec as P

EPSILON = 1e-05
HALF_ROOT = 0.7071067811865476
GAUSS_PEAK = 0.3989422804014327


def layer_norm(values):
    center = values - jnp.mean(values, axis=-1, keepdims=True)
    inv_scale = lax.rsqrt(jnp.mean(center * center, axis=-1, keepdims=True) + EPSILON)
    return (center * inv_scale, inv_scale)


def norm_backward(grad, normed, inv_scale):
    return inv_scale * (
        grad
        - jnp.mean(grad, axis=-1, keepdims=True)
        - normed * jnp.mean(grad * normed, axis=-1, keepdims=True)
    )


def gelu_value(values):
    return 0.5 * values * (1.0 + lax.erf(values * HALF_ROOT))


def gelu_slope(values):
    return (
        0.5 * (1.0 + lax.erf(values * HALF_ROOT))
        + values * jnp.exp(-0.5 * values * values) * GAUSS_PEAK
    )


MESH = pl.DeviceIdType.MESH
VMEM_LIMIT = 60 * 1024 * 1024


class Place:
    def __init__(self, groups):
        copy, shard = lax.axis_index("copy"), lax.axis_index("fsdp")
        self.groups = groups
        self.copy, self.shard = copy, shard
        self.x, self.h = copy // 2, copy % 2
        self.a, self.b = shard // 2, shard % 2
        self.core_peer = (self.x * 2 + 1 - self.h, shard)
        self.x_peer = ((1 - self.x) * 2 + self.h, shard)
        self.y_peer = (copy, self.a * 2 + 1 - self.b)

    def later(self, d):
        return lax.rem(self.a + d, self.groups)

    def earlier(self, d):
        return lax.rem(self.a + self.groups - d, self.groups)

    def z_peer(self, d):
        return (self.copy, self.later(d) * 2 + self.b)

    def greet(self):
        barrier = pltpu.get_barrier_semaphore()
        peers = [self.core_peer, self.x_peer, self.y_peer]
        peers += [self.z_peer(d) for d in range(1, self.groups)]
        for peer in peers:
            pl.semaphore_signal(barrier, inc=1, device_id=peer, device_id_type=MESH)
        pl.semaphore_wait(barrier, len(peers))


class Sender:
    def __init__(self, send_sem, recv_sem):
        self.send_sem, self.recv_sem, self.count, self.started = send_sem, recv_sem, 0, []

    def send(self, src, dst, peer):
        copy = pltpu.make_async_remote_copy(
            src_ref=src,
            dst_ref=dst,
            send_sem=self.send_sem.at[self.count],
            recv_sem=self.recv_sem.at[self.count],
            device_id=peer,
            device_id_type=MESH,
        )
        copy.start()
        self.count += 1
        self.started.append(copy)
        return copy

    def drain(self):
        for copy in self.started:
            copy.wait_send()


def columns(index, size):
    return pl.ds(pl.multiple_of(index * size, 128), size)


def wavefront(stages, count):
    for step in range(count + len(stages) - 1):
        for number, stage in reversed(list(enumerate(stages))):
            if 0 <= step - number < count:
                stage(step - number)


def gather_kernel(groups, quarter, w_in, w_out, conv, dec_out, dec_in, own_targets,
                  w_in_all, w_out_all, conv_all, dec_out_all, dec_in_all, targets,
                  send_sem, recv_sem, local_sem):
    at = Place(groups)
    a, b, h, x = at.a, at.b, at.h, at.x
    half = 2 * quarter
    sender = Sender(send_sem, recv_sem)
    ins = (w_in, w_out, conv, dec_out, dec_in)
    outs = (w_in_all, w_out_all, conv_all, dec_out_all, dec_in_all)
    split = (True, True, False, True, False)
    own = (
        w_in.at[h, x], w_out.at[h, x], conv.at[h], dec_out.at[:, columns(2 * h + x, quarter)], dec_in.at[h],
    )

    def piece(t, i, j):
        if t < 2:
            return outs[t].at[i, j, h, x]
        if t == 2:
            return outs[t].at[h, :, i, j]
        if t == 3:
            return outs[t].at[i, j, :, columns(2 * h + x, quarter)]
        return outs[t].at[i, j, h]

    def both(t, i):
        if t < 2:
            return outs[t].at[i, :, h, x]
        return outs[t].at[i, :, :, columns(2 * h + x, quarter)]

    def half_piece(t, i, j):
        if t == 3:
            return outs[t].at[i, j, :, columns(h, half)]
        if t < 2:
            return outs[t].at[i, j, h]
        return piece(t, i, j)

    def half_both(t, i):
        if t == 2:
            return outs[t].at[h, :, i]
        if t == 3:
            return outs[t].at[i, :, :, columns(h, half)]
        return outs[t].at[i, :, h]

    at.greet()
    locals_ = []
    for t in range(5):
        place = outs[t].at[:, :, a, b] if t == 2 else outs[t].at[a, b]
        locals_.append(pltpu.make_async_copy(ins[t], place, local_sem.at[t]))
    locals_.append(pltpu.make_async_copy(own_targets, targets.at[at.copy], local_sem.at[5]))
    for copy in locals_:
        copy.start()
    z_copies, y_copies, x_copies, core_copies = {}, {}, {}, {}
    for t in range(5):
        for d in range(1, groups):
            z_copies[t, d] = sender.send(own[t], piece(t, a, b), at.z_peer(d))
        y_copies[t, 0] = sender.send(own[t], piece(t, a, b), at.y_peer)
    target_x = sender.send(own_targets, targets.at[at.copy], at.x_peer)
    target_core = sender.send(own_targets, targets.at[at.copy], at.core_peer)

    def after_z(t):
        for d in range(1, groups):
            z_copies[t, d].wait_recv()
            block = piece(t, at.earlier(d), b)
            y_copies[t, d] = sender.send(block, block, at.y_peer)

    def after_y(t):
        for d in range(groups):
            y_copies[t, d].wait_recv()
            i = at.earlier(d)
            if split[t]:
                block = both(t, i) if d else piece(t, i, 1 - b)
                x_copies[t, d] = sender.send(block, block, at.x_peer)
            else:
                block = half_both(t, i) if d else half_piece(t, i, 1 - b)
                core_copies[t, d] = sender.send(block, block, at.core_peer)

    def after_x(t):
        if split[t]:
            for d in range(groups):
                x_copies[t, d].wait_recv()
                i = at.earlier(d)
                block = half_both(t, i) if d else half_piece(t, i, 1 - b)
                core_copies[t, d] = sender.send(block, block, at.core_peer)

    wavefront((after_z, after_y, after_x), 5)
    target_x.wait_recv()
    block = targets.at[at.x_peer[0]]
    target_last = sender.send(block, block, at.core_peer)
    for copy in core_copies.values():
        copy.wait_recv()
    target_core.wait_recv()
    target_last.wait_recv()
    sender.drain()
    for copy in locals_:
        copy.wait()


def gather_all(w_in, w_out, dec_in, dec_conv, dec_out, own_targets):
    shards, copies = lax.axis_size("fsdp"), lax.axis_size("copy")
    groups = shards // 2
    width, hidden = w_in.shape[0] * shards, w_in.shape[1]
    conv_rows, layers, kernel, channels = dec_conv.shape
    ins = (
        w_in.reshape(2, 2, -1, w_in.shape[1]),
        w_out.reshape(2, 2, -1, w_out.shape[1]),
        jnp.transpose(dec_conv, (1, 2, 0, 3)),
        dec_out,
        dec_in.reshape(2, -1, dec_in.shape[1]),
        own_targets.reshape(-1, own_targets.shape[-1]),
    )
    shapes = [(groups, 2) + ins[t].shape for t in (0, 1)]
    shapes.append((layers, kernel, groups, 2, conv_rows, channels))
    shapes += [(groups, 2) + ins[3].shape, (groups, 2) + ins[4].shape, (copies,) + ins[5].shape]
    count = 5 * groups + 5 * groups + 3 * groups + 3 + 2 * groups + 3 * groups
    sent = 2 * sum(math.prod(shape) for shape in shapes)
    outs = pl.pallas_call(
        lambda *refs: gather_kernel(groups, dec_out.shape[1] // 4, *refs),
        name="gather_weights",
        out_shape=[jax.ShapeDtypeStruct(shape, jnp.bfloat16) for shape in shapes],
        in_specs=[pl.BlockSpec(memory_space=pltpu.VMEM)] * 6,
        out_specs=[pl.BlockSpec(memory_space=pl.ANY)] * 6,
        scratch_shapes=[
            pltpu.SemaphoreType.DMA((count,)),
            pltpu.SemaphoreType.DMA((count,)),
            pltpu.SemaphoreType.DMA((6,)),
        ],
        compiler_params=pltpu.CompilerParams(
            collective_id=0, has_side_effects=True, vmem_limit_bytes=VMEM_LIMIT
        ),
        cost_estimate=pl.CostEstimate(flops=0, bytes_accessed=sent, transcendentals=0),
    )(*ins)
    return (
        outs[0].reshape(width, hidden),
        outs[1].reshape(hidden, width),
        outs[4].reshape(width, channels),
        outs[2].reshape(layers, kernel * channels, channels),
        outs[3].reshape(channels, width),
        outs[5],
    )


def reduce_kernel(groups, quarter, w_in, w_out, conv, dec_out, dec_in, loss,
                  w_in_sum, w_out_sum, conv_sum, dec_out_sum, dec_in_sum, loss_sum,
                  c0, c1, c2, c3, c4, x0, x1, x3, y0, y1, y2, y3, y4, z0, z1, z2, z3, z4,
                  f2, f4, e2, e4, lc, lcs, lx, lxs, ly, lys, lz, send_sem, recv_sem):
    at = Place(groups)
    a, b, h, x = at.a, at.b, at.h, at.x
    half = 2 * quarter
    sender = Sender(send_sem, recv_sem)
    ins = (w_in, w_out, conv, dec_out, dec_in)
    outs = (w_in_sum, w_out_sum, conv_sum, dec_out_sum, dec_in_sum)
    rc, rx, ry, rz = (c0, c1, c2, c3, c4), (x0, x1, None, x3, None), (y0, y1, y2, y3, y4), (z0, z1, z2, z3, z4)
    first, other = (None, None, f2, None, f4), (None, None, e2, None, e4)
    split = (True, True, False, True, False)

    def plus(left, right):
        return (left.astype(jnp.float32) + right.astype(jnp.float32)).astype(jnp.bfloat16)

    def each(total, body):
        def step(i, carry):
            body(i)
            return carry

        lax.fori_loop(0, total, step, 0)

    at.greet()
    copies = {}
    for t in range(5):
        if t == 2:
            source = ins[t].at[1 - h]
        elif t == 3:
            source = ins[t].at[:, :, :, columns(1 - h, half)]
        else:
            source = ins[t].at[:, :, 1 - h]
        copies["c", t] = sender.send(source, rc[t], at.core_peer)
        if t == 0:
            copies["c", 5] = sender.send(loss, lc, at.core_peer)

    def after_core(t):
        copies["c", t].wait_recv()
        if t == 5:
            lcs[...] = loss[...] + lc[...]
            copies["x", t] = sender.send(lcs, lx, at.x_peer)
            return
        c, g = rc[t], ins[t]

        def body(i):
            if t == 2:
                c[i] = plus(c[i], g[h, i])
            elif t == 3:
                c[i] = plus(c[i], g[i, :, :, columns(h, half)])
            else:
                c[i] = plus(c[i], g[i, :, h])

        each(c.shape[0], body)
        if t < 2:
            copies["x", t] = sender.send(c.at[:, :, 1 - x], rx[t], at.x_peer)
        elif t == 3:
            copies["x", t] = sender.send(c.at[:, :, :, columns(1 - x, quarter)], rx[t], at.x_peer)

    def after_x(t):
        if t == 5:
            copies["x", t].wait_recv()
            lxs[...] = lcs[...] + lx[...]
            copies["y", t] = sender.send(lxs, ly, at.y_peer)
            return
        current = rc[t]
        if split[t]:
            copies["x", t].wait_recv()
            c, r = rc[t], rx[t]

            def body(i):
                if t == 3:
                    r[i] = plus(r[i], c[i, :, :, columns(x, quarter)])
                else:
                    r[i] = plus(r[i], c[i, :, x])

            each(groups, body)
            current = r
        source = current.at[:, :, 1 - b] if t == 2 else current.at[:, 1 - b]
        copies["y", t] = sender.send(source, ry[t], at.y_peer)

    def after_y(t):
        copies["y", t].wait_recv()
        if t == 5:
            lys[...] = lxs[...] + ly[...]
            lz[a] = lys[...]
            for d in range(1, groups):
                copies["z", t, d] = sender.send(lys, lz.at[a], at.z_peer(d))
            return
        current = rx[t] if split[t] else rc[t]
        r = ry[t]

        def body(i):
            if t == 2:
                r[i] = plus(r[i], current[i, :, b])
            else:
                r[i] = plus(r[i], current[i, b])

        each(r.shape[0], body)
        for d in range(1, groups):
            source = r.at[:, at.later(d)] if t == 2 else r.at[at.later(d)]
            copies["z", t, d] = sender.send(source, rz[t].at[d - 1], at.z_peer(d))

    def after_z(t):
        for d in range(1, groups):
            copies["z", t, d].wait_recv()
        if t == 5:
            total = lz[0]
            for i in range(1, groups):
                total = total + lz[i]
            loss_sum[...] = total
            return
        r = rz[t]
        total = (ry[t][:, a] if t == 2 else ry[t][a]).astype(jnp.float32)
        for d in range(1, groups):
            total = total + r[d - 1].astype(jnp.float32)
        total = total.astype(jnp.bfloat16)
        if t < 2:
            outs[t][h, x] = total
            block = outs[t].at[h, x]
            copies["e", t] = sender.send(block, block, at.x_peer)
        elif t == 3:
            outs[t][:, columns(2 * h + x, quarter)] = total
            block = outs[t].at[:, columns(2 * h + x, quarter)]
            copies["e", t] = sender.send(block, block, at.x_peer)
        else:
            first[t][...] = total
            copies["e", t] = sender.send(first[t], other[t], at.x_peer)

    def after_exchange(t):
        if t == 5:
            return
        copies["e", t].wait_recv()
        if not split[t]:
            outs[t][h] = plus(first[t][...], other[t][...])
        block = outs[t].at[:, columns(h, half)] if t == 3 else outs[t].at[h]
        copies["f", t] = sender.send(block, block, at.core_peer)

    wavefront((after_core, after_x, after_y, after_z, after_exchange), 6)
    for t in range(5):
        copies["f", t].wait_recv()
    sender.drain()


def reduce_all(in_proj, out_proj, dec_in, conv, dec_out, loss):
    shards = lax.axis_size("fsdp")
    groups = shards // 2
    rows_in, rows_out, rows_dec = in_proj.shape[0] // shards, out_proj.shape[0] // shards, dec_out.shape[0] // shards
    layers, taps, channels = conv.shape[0], conv.shape[1], conv.shape[3]
    hidden, width = in_proj.shape[1], out_proj.shape[1]
    quarter = width // 4
    q_in, q_out, half_dec = rows_in // 4, rows_out // 4, rows_in // 2
    ins = (
        in_proj.reshape(groups, 2, 2, 2, q_in, hidden),
        out_proj.reshape(groups, 2, 2, 2, q_out, width),
        conv.reshape(layers, taps, groups, 2, rows_dec, channels),
        dec_out.reshape(groups, 2, rows_dec, width),
        dec_in.reshape(groups, 2, 2, half_dec, channels),
        loss,
    )
    outs = (
        (2, 2, q_in, hidden), (2, 2, q_out, width), (layers, taps, rows_dec, channels),
        (rows_dec, width), (2, half_dec, channels),
    )
    half_shapes = (
        (groups, 2, 2, q_in, hidden), (groups, 2, 2, q_out, width), (taps, groups, 2, rows_dec, channels),
        (groups, 2, rows_dec, 2 * quarter), (groups, 2, half_dec, channels),
    )
    x_shapes = ((groups, 2, q_in, hidden), (groups, 2, q_out, width), (groups, 2, rows_dec, quarter))
    last = ((q_in, hidden), (q_out, width), (taps, rows_dec, channels), (rows_dec, quarter), (half_dec, channels))
    y_shapes = ((groups,) + last[0], (groups,) + last[1], (taps, groups, rows_dec, channels), (groups,) + last[3], (groups,) + last[4])
    z_shapes = tuple((groups - 1,) + shape for shape in last)
    scratch = half_shapes + x_shapes + y_shapes + z_shapes + (last[2], last[4], last[2], last[4])
    count = 6 + 4 + 6 + 6 * (groups - 1) + 5 + 5
    tile = loss.shape
    sums = pl.pallas_call(
        lambda *refs: reduce_kernel(groups, quarter, *refs),
        name="reduce_grads",
        out_shape=[jax.ShapeDtypeStruct(shape, jnp.bfloat16) for shape in outs]
        + [jax.ShapeDtypeStruct(tile, jnp.float32)],
        in_specs=[pl.BlockSpec(memory_space=pltpu.VMEM)] * 6,
        out_specs=[pl.BlockSpec(memory_space=pltpu.VMEM)] * 6,
        scratch_shapes=[pltpu.VMEM(shape, jnp.bfloat16) for shape in scratch]
        + [pltpu.VMEM(tile, jnp.float32)] * 6
        + [pltpu.VMEM((groups,) + tile, jnp.float32)]
        + [pltpu.SemaphoreType.DMA((count,)), pltpu.SemaphoreType.DMA((count,))],
        compiler_params=pltpu.CompilerParams(
            collective_id=1, has_side_effects=True, vmem_limit_bytes=VMEM_LIMIT
        ),
    )(*ins)
    return (
        sums[0].reshape(rows_in, hidden),
        sums[1].reshape(rows_out, width),
        sums[4].reshape(rows_in, channels),
        jnp.transpose(sums[2], (2, 0, 1, 3)),
        sums[3],
        sums[5][0, 0],
    )


def unfold_frames(state, width):
    half = width // 2
    frames = state.shape[1]
    padded = jnp.pad(state, ((0, 0), (half, half), (0, 0)))
    return jnp.concatenate([padded[:, k : k + frames] for k in range(width)], axis=-1)


def fold_frames(grad, width, channels):
    units, frames = (grad.shape[0], grad.shape[1])
    half = width // 2
    split_grad = grad.reshape(units, frames, width, channels)
    padded = jnp.pad(split_grad, ((0, 0), (half, half), (0, 0), (0, 0)))
    total = jnp.zeros((units, frames, channels), grad.dtype)
    for k in range(width):
        total = total + padded[:, 2 * half - k : 2 * half - k + frames, k]
    return total


def teacher_targets(layer_outputs, lengths):
    frames = layer_outputs.shape[2]
    valid = (jnp.arange(frames, dtype=jnp.int32)[None, :] < lengths[:, None]).astype(jnp.float32)
    weight = valid[:, :, None]
    count = jnp.sum(valid, axis=1)[:, None, None]
    total = jnp.zeros(layer_outputs.shape[1:], jnp.float32)
    for k in range(layer_outputs.shape[0]):
        values = layer_outputs[k].astype(jnp.float32)
        mean = jnp.sum(values * weight, axis=1, keepdims=True) / count
        center = values - mean
        variance = jnp.sum(center * center * weight, axis=1, keepdims=True) / count
        total = total + center * lax.rsqrt(variance + EPSILON)
    return (total * weight / layer_outputs.shape[0]).astype(jnp.bfloat16)


def contract_rows(left, right):
    return lax.dot_general(
        left, right, (((0,), (0,)), ((), ())), preferred_element_type=jnp.float32
    )


def contract_cols(left, right):
    return lax.dot_general(
        left, right, (((1,), (1,)), ((), ())), preferred_element_type=jnp.float32
    )


def on_device(
    student_hidden, keep_index, lengths, teacher_layers, w_in, w_out, dec_in, dec_conv, dec_out
):
    copy_index = lax.axis_index("copy")
    units, keep_count, width = (
        student_hidden.shape[1],
        student_hidden.shape[2],
        student_hidden.shape[3],
    )
    frames = teacher_layers.shape[3]
    per_copy = teacher_layers.shape[2]
    layers = dec_conv.shape[1]
    kernel = dec_conv.shape[2]
    channels = dec_conv.shape[3]
    rows = units * keep_count
    masked_count = frames - keep_count
    frame_index = jnp.arange(frames, dtype=jnp.int32)
    valid = frame_index[None, :] < lengths[:, None]
    own_keep = lax.dynamic_index_in_dim(keep_index, copy_index, 0, keepdims=False)
    chosen = own_keep[:, None, :] == frame_index[None, :, None]
    own_kept = jnp.any(chosen, axis=2)
    select = chosen.astype(jnp.bfloat16)
    masked = jnp.logical_and(valid, jnp.logical_not(own_kept)).astype(jnp.float32)
    own_lengths = lax.dynamic_slice_in_dim(lengths, copy_index * per_copy, per_copy, 0)
    own_targets = teacher_targets(teacher_layers[:, 0], own_lengths)
    hidden_rows = student_hidden[0].reshape(rows, width).astype(jnp.float32)
    normed_exact, inv_scale = layer_norm(hidden_rows)
    normed = normed_exact.astype(jnp.bfloat16)
    w_in_all, w_out_all, dec_in_all, dec_conv_all, dec_out_all, targets = gather_all(
        w_in, w_out, dec_in, dec_conv, dec_out, own_targets
    )
    projected = jnp.dot(normed, w_in_all, preferred_element_type=jnp.float32)
    activation = gelu_value(projected).astype(jnp.bfloat16)
    mixed = jnp.dot(activation, w_out_all, preferred_element_type=jnp.float32)
    student_out = (hidden_rows + mixed).astype(jnp.bfloat16)
    lifted = jnp.dot(student_out, dec_in_all, preferred_element_type=jnp.float32).astype(
        jnp.bfloat16
    )
    state = jnp.einsum(
        "utk,ukc->utc",
        select,
        lifted.reshape(units, keep_count, channels),
        preferred_element_type=jnp.float32,
    ).astype(jnp.bfloat16)
    saved = []
    for layer in range(layers):
        unfolded = unfold_frames(state, kernel).reshape(units * frames, kernel * channels)
        convolved = jnp.dot(
            unfolded, dec_conv_all[layer], preferred_element_type=jnp.float32
        )
        conv_normed, conv_scale = layer_norm(convolved)
        result = gelu_value(conv_normed)
        if layer > 0:
            result = result + state.reshape(units * frames, channels).astype(jnp.float32)
        saved.append((unfolded, conv_normed, conv_scale))
        state = result.reshape(units, frames, channels).astype(jnp.bfloat16)
    final_state = state.reshape(units * frames, channels)
    prediction = jnp.dot(final_state, dec_out_all, preferred_element_type=jnp.float32)
    loss_scale = 1.0 / math.sqrt(width)
    error = (
        prediction - targets.reshape(units * frames, width).astype(jnp.float32)
    ) * masked.reshape(units * frames, 1)
    total = jnp.sum(error * error) * loss_scale
    prediction_grad = (2.0 * loss_scale * error).astype(jnp.bfloat16)
    out_term = contract_rows(final_state, prediction_grad)
    state_grad = contract_cols(prediction_grad, dec_out_all)
    kernel_terms = [None] * layers
    for layer in reversed(range(layers)):
        unfolded, conv_normed, conv_scale = saved[layer]
        filter_grad = norm_backward(
            state_grad * gelu_slope(conv_normed), conv_normed, conv_scale
        ).astype(jnp.bfloat16)
        kernel_terms[layer] = contract_rows(unfolded, filter_grad)
        unfold_grad = contract_cols(filter_grad, dec_conv_all[layer])
        previous_grad = fold_frames(
            unfold_grad.reshape(units, frames, kernel * channels), kernel, channels
        ).reshape(units * frames, channels)
        if layer > 0:
            previous_grad = previous_grad + state_grad
        state_grad = previous_grad
    conv_term = jnp.stack(
        [term.reshape(kernel, channels, channels).astype(jnp.bfloat16) for term in kernel_terms]
    )
    lifted_grad = (
        jnp.einsum(
            "utk,utc->ukc",
            select,
            state_grad.reshape(units, frames, channels).astype(jnp.bfloat16),
            preferred_element_type=jnp.float32,
        )
        .reshape(rows, channels)
        .astype(jnp.bfloat16)
    )
    in_term = contract_rows(student_out, lifted_grad)
    output_grad = contract_cols(lifted_grad, dec_in_all)
    output_half = output_grad.astype(jnp.bfloat16)
    activation_grad = contract_cols(output_half, w_out_all)
    projected_grad = (activation_grad * gelu_slope(projected)).astype(jnp.bfloat16)
    normed_grad = contract_cols(projected_grad, w_in_all)
    grad_hidden = (output_grad + norm_backward(normed_grad, normed_exact, inv_scale)).astype(
        jnp.bfloat16
    )
    *summed, loss_total = reduce_all(
        contract_rows(normed, projected_grad).astype(jnp.bfloat16),
        contract_rows(activation, output_half).astype(jnp.bfloat16),
        in_term.astype(jnp.bfloat16),
        conv_term,
        out_term.astype(jnp.bfloat16),
        jnp.full((8, 128), total, jnp.float32),
    )
    slot_total = lax.axis_size("copy") * lax.axis_size("fsdp") * units * masked_count
    loss = loss_total / float(slot_total)
    return (
        loss,
        grad_hidden.reshape(1, units, keep_count, width),
        *summed,
    )


def solution(mesh):
    placed = (
        P("copy", "fsdp", None, None),
        P(None, "fsdp", None),
        P("fsdp"),
        P(None, "copy", "fsdp", None, None),
        P("fsdp", None),
        P("fsdp", None),
        P("fsdp", None),
        P("fsdp", None, None, None),
        P("fsdp", None),
    )
    return jax.shard_map(
        on_device,
        mesh=mesh,
        in_specs=placed,
        out_specs=(
            P(),
            P("copy", "fsdp", None, None),
            P("fsdp", None),
            P("fsdp", None),
            P("fsdp", None),
            P("fsdp", None, None, None),
            P("fsdp", None),
        ),
        check_vma=False,
    )
```

```python
import math

import jax
import jax.numpy as jnp
from jax import lax
from jax.experimental import pallas as pl
from jax.experimental.pallas import tpu as pltpu
from jax.sharding import PartitionSpec as P

EPSILON = 1e-05
HALF_ROOT = 0.7071067811865476
GAUSS_PEAK = 0.3989422804014327


def layer_norm(values):
    center = values - jnp.mean(values, axis=-1, keepdims=True)
    inv_scale = lax.rsqrt(jnp.mean(center * center, axis=-1, keepdims=True) + EPSILON)
    return (center * inv_scale, inv_scale)


def norm_backward(grad, normed, inv_scale):
    return inv_scale * (
        grad
        - jnp.mean(grad, axis=-1, keepdims=True)
        - normed * jnp.mean(grad * normed, axis=-1, keepdims=True)
    )


def gelu_value(values):
    return 0.5 * values * (1.0 + lax.erf(values * HALF_ROOT))


def gelu_slope(values):
    return (
        0.5 * (1.0 + lax.erf(values * HALF_ROOT))
        + values * jnp.exp(-0.5 * values * values) * GAUSS_PEAK
    )


MESH = pl.DeviceIdType.MESH
VMEM_LIMIT = 60 * 1024 * 1024


class Place:
    def __init__(self, groups):
        copy, shard = lax.axis_index("copy"), lax.axis_index("fsdp")
        self.groups = groups
        self.copy, self.shard = copy, shard
        self.x, self.h = copy // 2, copy % 2
        self.a, self.b = shard // 2, shard % 2
        self.core_peer = (self.x * 2 + 1 - self.h, shard)
        self.x_peer = ((1 - self.x) * 2 + self.h, shard)
        self.y_peer = (copy, self.a * 2 + 1 - self.b)

    def later(self, d):
        return lax.rem(self.a + d, self.groups)

    def earlier(self, d):
        return lax.rem(self.a + self.groups - d, self.groups)

    def z_peer(self, d):
        return (self.copy, self.later(d) * 2 + self.b)

    def greet(self):
        barrier = pltpu.get_barrier_semaphore()
        peers = [self.core_peer, self.x_peer, self.y_peer]
        peers += [self.z_peer(d) for d in range(1, self.groups)]
        for peer in peers:
            pl.semaphore_signal(barrier, inc=1, device_id=peer, device_id_type=MESH)
        pl.semaphore_wait(barrier, len(peers))


class Sender:
    def __init__(self, send_sem, recv_sem):
        self.send_sem, self.recv_sem, self.count, self.started = send_sem, recv_sem, 0, []

    def send(self, src, dst, peer):
        copy = pltpu.make_async_remote_copy(
            src_ref=src,
            dst_ref=dst,
            send_sem=self.send_sem.at[self.count],
            recv_sem=self.recv_sem.at[self.count],
            device_id=peer,
            device_id_type=MESH,
        )
        copy.start()
        self.count += 1
        self.started.append(copy)
        return copy

    def drain(self):
        for copy in self.started:
            copy.wait_send()


def columns(index, size):
    return pl.ds(pl.multiple_of(index * size, 128), size)


def wavefront(stages, count):
    for step in range(count + stages[-1][0]):
        for lag, stage in reversed(stages):
            if 0 <= step - lag < count:
                stage(step - lag)


def gather_kernel(groups, quarter, w_in, w_out, conv, dec_out, dec_in, own_targets,
                  w_in_all, w_out_all, conv_all, dec_out_all, dec_in_all, targets,
                  send_sem, recv_sem, local_sem):
    at = Place(groups)
    a, b, h, x = at.a, at.b, at.h, at.x
    half = 2 * quarter
    sender = Sender(send_sem, recv_sem)
    ins = (w_in, w_out, conv, dec_out, dec_in)
    outs = (w_in_all, w_out_all, conv_all, dec_out_all, dec_in_all)
    split = (True, True, False, True, False)
    own = (
        w_in.at[h, x], w_out.at[h, x], conv.at[h], dec_out.at[:, columns(2 * h + x, quarter)], dec_in.at[h],
    )

    def piece(t, i, j):
        if t < 2:
            return outs[t].at[i, j, h, x]
        if t == 2:
            return outs[t].at[h, :, i, j]
        if t == 3:
            return outs[t].at[i, j, :, columns(2 * h + x, quarter)]
        return outs[t].at[i, j, h]

    def both(t, i):
        if t < 2:
            return outs[t].at[i, :, h, x]
        return outs[t].at[i, :, :, columns(2 * h + x, quarter)]

    def half_piece(t, i, j):
        if t == 3:
            return outs[t].at[i, j, :, columns(h, half)]
        if t < 2:
            return outs[t].at[i, j, h]
        return piece(t, i, j)

    def half_both(t, i):
        if t == 2:
            return outs[t].at[h, :, i]
        if t == 3:
            return outs[t].at[i, :, :, columns(h, half)]
        return outs[t].at[i, :, h]

    at.greet()
    locals_ = []
    for t in range(5):
        place = outs[t].at[:, :, a, b] if t == 2 else outs[t].at[a, b]
        locals_.append(pltpu.make_async_copy(ins[t], place, local_sem.at[t]))
    locals_.append(pltpu.make_async_copy(own_targets, targets.at[at.copy], local_sem.at[5]))
    for copy in locals_:
        copy.start()
    order = (0, 2, 1, 3, 4)
    chunks = [(t, d) for d in range(groups) for t in order]
    z_copies, y_copies, x_copies, core_copies = {}, {}, {}, {}
    for t in order:
        y_copies[t, 0] = sender.send(own[t], piece(t, a, b), at.y_peer)
        if groups > 1:
            z_copies[t, 1] = sender.send(own[t], piece(t, a, b), at.z_peer(1))
    for t, d in chunks:
        if d > 1:
            z_copies[t, d] = sender.send(own[t], piece(t, a, b), at.z_peer(d))
    target_x = sender.send(own_targets, targets.at[at.copy], at.x_peer)
    target_core = sender.send(own_targets, targets.at[at.copy], at.core_peer)

    def after_z(c):
        t, d = chunks[c]
        if d:
            z_copies[t, d].wait_recv()
            block = piece(t, at.earlier(d), b)
            y_copies[t, d] = sender.send(block, block, at.y_peer)

    def after_y(c):
        t, d = chunks[c]
        y_copies[t, d].wait_recv()
        i = at.earlier(d)
        if split[t]:
            block = both(t, i) if d else piece(t, i, 1 - b)
            x_copies[t, d] = sender.send(block, block, at.x_peer)
        else:
            block = half_both(t, i) if d else half_piece(t, i, 1 - b)
            core_copies[t, d] = sender.send(block, block, at.core_peer)

    def after_x(c):
        t, d = chunks[c]
        if split[t]:
            x_copies[t, d].wait_recv()
            i = at.earlier(d)
            block = half_both(t, i) if d else half_piece(t, i, 1 - b)
            core_copies[t, d] = sender.send(block, block, at.core_peer)

    wavefront(((0, after_z), (3, after_y), (6, after_x)), len(chunks))
    target_x.wait_recv()
    block = targets.at[at.x_peer[0]]
    target_last = sender.send(block, block, at.core_peer)
    for copy in core_copies.values():
        copy.wait_recv()
    target_core.wait_recv()
    target_last.wait_recv()
    sender.drain()
    for copy in locals_:
        copy.wait()


def gather_all(w_in, w_out, dec_in, dec_conv, dec_out, own_targets):
    shards, copies = lax.axis_size("fsdp"), lax.axis_size("copy")
    groups = shards // 2
    width, hidden = w_in.shape[0] * shards, w_in.shape[1]
    conv_rows, layers, kernel, channels = dec_conv.shape
    ins = (
        w_in.reshape(2, 2, -1, w_in.shape[1]),
        w_out.reshape(2, 2, -1, w_out.shape[1]),
        jnp.transpose(dec_conv, (1, 2, 0, 3)),
        dec_out,
        dec_in.reshape(2, -1, dec_in.shape[1]),
        own_targets.reshape(-1, own_targets.shape[-1]),
    )
    shapes = [(groups, 2) + ins[t].shape for t in (0, 1)]
    shapes.append((layers, kernel, groups, 2, conv_rows, channels))
    shapes += [(groups, 2) + ins[3].shape, (groups, 2) + ins[4].shape, (copies,) + ins[5].shape]
    count = 5 * groups + 5 * groups + 3 * groups + 3 + 2 * groups + 3 * groups
    sent = 2 * sum(math.prod(shape) for shape in shapes)
    outs = pl.pallas_call(
        lambda *refs: gather_kernel(groups, dec_out.shape[1] // 4, *refs),
        name="gather_weights",
        out_shape=[jax.ShapeDtypeStruct(shape, jnp.bfloat16) for shape in shapes],
        in_specs=[pl.BlockSpec(memory_space=pltpu.VMEM)] * 6,
        out_specs=[pl.BlockSpec(memory_space=pl.ANY)] * 6,
        scratch_shapes=[
            pltpu.SemaphoreType.DMA((count,)),
            pltpu.SemaphoreType.DMA((count,)),
            pltpu.SemaphoreType.DMA((6,)),
        ],
        compiler_params=pltpu.CompilerParams(
            collective_id=0, has_side_effects=True, vmem_limit_bytes=VMEM_LIMIT
        ),
        cost_estimate=pl.CostEstimate(flops=0, bytes_accessed=sent, transcendentals=0),
    )(*ins)
    return (
        outs[0].reshape(width, hidden),
        outs[1].reshape(hidden, width),
        outs[4].reshape(width, channels),
        outs[2].reshape(layers, kernel * channels, channels),
        outs[3].reshape(channels, width),
        outs[5],
    )


def reduce_kernel(groups, quarter, w_in, w_out, conv, dec_out, dec_in, loss,
                  w_in_sum, w_out_sum, conv_sum, dec_out_sum, dec_in_sum, loss_sum,
                  c0, c1, c2, c3, c4, x0, x1, x3, y0, y1, y2, y3, y4, z0, z1, z2, z3, z4,
                  f2, f4, e2, e4, lc, lcs, lx, lxs, ly, lys, lz, send_sem, recv_sem):
    at = Place(groups)
    a, b, h, x = at.a, at.b, at.h, at.x
    half = 2 * quarter
    sender = Sender(send_sem, recv_sem)
    ins = (w_in, w_out, conv, dec_out, dec_in)
    outs = (w_in_sum, w_out_sum, conv_sum, dec_out_sum, dec_in_sum)
    rc, rx, ry, rz = (c0, c1, c2, c3, c4), (x0, x1, None, x3, None), (y0, y1, y2, y3, y4), (z0, z1, z2, z3, z4)
    first, other = (None, None, f2, None, f4), (None, None, e2, None, e4)
    split = (True, True, False, True, False)

    def plus(left, right):
        return (left.astype(jnp.float32) + right.astype(jnp.float32)).astype(jnp.bfloat16)

    def each(total, body):
        def step(i, carry):
            body(i)
            return carry

        lax.fori_loop(0, total, step, 0)

    distances = tuple(range(1, groups)) + (0,)
    chunks = [(t, d) for part in ((0, 2), (1, 3, 4)) for d in distances for t in part]
    chunks.insert(2, (5, 0))
    at.greet()
    copies = {}
    for t, d in chunks:
        i = at.later(d)
        if t == 5:
            copies["c", t, d] = sender.send(loss, lc, at.core_peer)
        elif t == 2:
            copies["c", t, d] = sender.send(ins[t].at[1 - h, :, i], rc[t].at[:, i], at.core_peer)
        elif t == 3:
            source = ins[t].at[i, :, :, columns(1 - h, half)]
            copies["c", t, d] = sender.send(source, rc[t].at[i], at.core_peer)
        else:
            copies["c", t, d] = sender.send(ins[t].at[i, :, 1 - h], rc[t].at[i], at.core_peer)

    def send_y(t, d):
        i = at.later(d)
        current = rx[t] if split[t] else rc[t]
        if t == 2:
            copies["y", t, d] = sender.send(current.at[:, i, 1 - b], ry[t].at[:, i], at.y_peer)
        else:
            copies["y", t, d] = sender.send(current.at[i, 1 - b], ry[t].at[i], at.y_peer)

    def after_core(index):
        t, d = chunks[index]
        copies["c", t, d].wait_recv()
        if t == 5:
            lcs[...] = loss[...] + lc[...]
            copies["x", t, d] = sender.send(lcs, lx, at.x_peer)
            return
        c, g, i = rc[t], ins[t], at.later(d)
        if t < 2:

            def body(k):
                j, q = k // 2, k % 2
                c[i, j, q] = plus(c[i, j, q], g[i, j, h, q])

            each(4, body)
            copies["x", t, d] = sender.send(c.at[i, :, 1 - x], rx[t].at[i], at.x_peer)
        elif t == 2:

            def body(k):
                c[k, i] = plus(c[k, i], g[h, k, i])

            each(c.shape[0], body)
            send_y(t, d)
        elif t == 3:
            c[i] = plus(c[i], g[i, :, :, columns(h, half)])
            source = c.at[i, :, :, columns(1 - x, quarter)]
            copies["x", t, d] = sender.send(source, rx[t].at[i], at.x_peer)
        else:
            c[i] = plus(c[i], g[i, :, h])
            send_y(t, d)

    def after_x(index):
        t, d = chunks[index]
        if t == 5:
            copies["x", t, d].wait_recv()
            lxs[...] = lcs[...] + lx[...]
            copies["y", t, d] = sender.send(lxs, ly, at.y_peer)
        elif split[t]:
            copies["x", t, d].wait_recv()
            c, r, i = rc[t], rx[t], at.later(d)
            if t == 3:
                r[i] = plus(r[i], c[i, :, :, columns(x, quarter)])
            else:

                def body(k):
                    r[i, k] = plus(r[i, k], c[i, k, x])

                each(2, body)
            send_y(t, d)

    def after_y(index):
        t, d = chunks[index]
        copies["y", t, d].wait_recv()
        if t == 5:
            lys[...] = lxs[...] + ly[...]
            lz[a] = lys[...]
            for e in range(1, groups):
                copies["z", t, e] = sender.send(lys, lz.at[a], at.z_peer(e))
            return
        current = rx[t] if split[t] else rc[t]
        r, i = ry[t], at.later(d)
        if t == 2:

            def body(k):
                r[k, i] = plus(r[k, i], current[k, i, b])

            each(r.shape[0], body)
        else:
            r[i] = plus(r[i], current[i, b])
        if d:
            source = r.at[:, i] if t == 2 else r.at[i]
            copies["z", t, d] = sender.send(source, rz[t].at[d - 1], at.z_peer(d))

    def after_z(index):
        t, d = chunks[index]
        if t == 5:
            for e in range(1, groups):
                copies["z", t, e].wait_recv()
            total = lz[0]
            for i in range(1, groups):
                total = total + lz[i]
            loss_sum[...] = total
            return
        if d:
            return
        for e in range(1, groups):
            copies["z", t, e].wait_recv()
        r = rz[t]
        total = (ry[t][:, a] if t == 2 else ry[t][a]).astype(jnp.float32)
        for e in range(1, groups):
            total = total + r[e - 1].astype(jnp.float32)
        total = total.astype(jnp.bfloat16)
        if t < 2:
            outs[t][h, x] = total
            block = outs[t].at[h, x]
            copies["e", t] = sender.send(block, block, at.x_peer)
        elif t == 3:
            outs[t][:, columns(2 * h + x, quarter)] = total
            block = outs[t].at[:, columns(2 * h + x, quarter)]
            copies["e", t] = sender.send(block, block, at.x_peer)
        else:
            first[t][...] = total
            copies["e", t] = sender.send(first[t], other[t], at.x_peer)

    def after_exchange(index):
        t, d = chunks[index]
        if t == 5 or d:
            return
        copies["e", t].wait_recv()
        if not split[t]:
            outs[t][h] = plus(first[t][...], other[t][...])
        block = outs[t].at[:, columns(h, half)] if t == 3 else outs[t].at[h]
        copies["f", t] = sender.send(block, block, at.core_peer)

    wavefront(
        ((0, after_core), (2, after_x), (4, after_y), (6, after_z), (8, after_exchange)), len(chunks)
    )
    for t in range(5):
        copies["f", t].wait_recv()
    sender.drain()


def reduce_all(in_proj, out_proj, dec_in, conv, dec_out, loss):
    shards = lax.axis_size("fsdp")
    groups = shards // 2
    rows_in, rows_out, rows_dec = in_proj.shape[0] // shards, out_proj.shape[0] // shards, dec_out.shape[0] // shards
    layers, taps, channels = conv.shape[0], conv.shape[1], conv.shape[3]
    hidden, width = in_proj.shape[1], out_proj.shape[1]
    quarter = width // 4
    q_in, q_out, half_dec = rows_in // 4, rows_out // 4, rows_in // 2
    ins = (
        in_proj.reshape(groups, 2, 2, 2, q_in, hidden),
        out_proj.reshape(groups, 2, 2, 2, q_out, width),
        conv.reshape(layers, taps, groups, 2, rows_dec, channels),
        dec_out.reshape(groups, 2, rows_dec, width),
        dec_in.reshape(groups, 2, 2, half_dec, channels),
        loss,
    )
    outs = (
        (2, 2, q_in, hidden), (2, 2, q_out, width), (layers, taps, rows_dec, channels),
        (rows_dec, width), (2, half_dec, channels),
    )
    half_shapes = (
        (groups, 2, 2, q_in, hidden), (groups, 2, 2, q_out, width), (taps, groups, 2, rows_dec, channels),
        (groups, 2, rows_dec, 2 * quarter), (groups, 2, half_dec, channels),
    )
    x_shapes = ((groups, 2, q_in, hidden), (groups, 2, q_out, width), (groups, 2, rows_dec, quarter))
    last = ((q_in, hidden), (q_out, width), (taps, rows_dec, channels), (rows_dec, quarter), (half_dec, channels))
    y_shapes = ((groups,) + last[0], (groups,) + last[1], (taps, groups, rows_dec, channels), (groups,) + last[3], (groups,) + last[4])
    z_shapes = tuple((groups - 1,) + shape for shape in last)
    scratch = half_shapes + x_shapes + y_shapes + z_shapes + (last[2], last[4], last[2], last[4])
    count = (5 + 3 + 5) * groups + 3 + 6 * (groups - 1) + 5 + 5
    tile = loss.shape
    sums = pl.pallas_call(
        lambda *refs: reduce_kernel(groups, quarter, *refs),
        name="reduce_grads",
        out_shape=[jax.ShapeDtypeStruct(shape, jnp.bfloat16) for shape in outs]
        + [jax.ShapeDtypeStruct(tile, jnp.float32)],
        in_specs=[pl.BlockSpec(memory_space=pltpu.VMEM)] * 6,
        out_specs=[pl.BlockSpec(memory_space=pltpu.VMEM)] * 6,
        scratch_shapes=[pltpu.VMEM(shape, jnp.bfloat16) for shape in scratch]
        + [pltpu.VMEM(tile, jnp.float32)] * 6
        + [pltpu.VMEM((groups,) + tile, jnp.float32)]
        + [pltpu.SemaphoreType.DMA((count,)), pltpu.SemaphoreType.DMA((count,))],
        compiler_params=pltpu.CompilerParams(
            collective_id=1, has_side_effects=True, vmem_limit_bytes=VMEM_LIMIT
        ),
    )(*ins)
    return (
        sums[0].reshape(rows_in, hidden),
        sums[1].reshape(rows_out, width),
        sums[4].reshape(rows_in, channels),
        jnp.transpose(sums[2], (2, 0, 1, 3)),
        sums[3],
        sums[5][0, 0],
    )


def unfold_frames(state, width):
    half = width // 2
    frames = state.shape[1]
    padded = jnp.pad(state, ((0, 0), (half, half), (0, 0)))
    return jnp.concatenate([padded[:, k : k + frames] for k in range(width)], axis=-1)


def fold_frames(grad, width, channels):
    units, frames = (grad.shape[0], grad.shape[1])
    half = width // 2
    split_grad = grad.reshape(units, frames, width, channels)
    padded = jnp.pad(split_grad, ((0, 0), (half, half), (0, 0), (0, 0)))
    total = jnp.zeros((units, frames, channels), grad.dtype)
    for k in range(width):
        total = total + padded[:, 2 * half - k : 2 * half - k + frames, k]
    return total


def teacher_targets(layer_outputs, lengths):
    frames = layer_outputs.shape[2]
    valid = (jnp.arange(frames, dtype=jnp.int32)[None, :] < lengths[:, None]).astype(jnp.float32)
    weight = valid[:, :, None]
    count = jnp.sum(valid, axis=1)[:, None, None]
    total = jnp.zeros(layer_outputs.shape[1:], jnp.float32)
    for k in range(layer_outputs.shape[0]):
        values = layer_outputs[k].astype(jnp.float32)
        mean = jnp.sum(values * weight, axis=1, keepdims=True) / count
        center = values - mean
        variance = jnp.sum(center * center * weight, axis=1, keepdims=True) / count
        total = total + center * lax.rsqrt(variance + EPSILON)
    return (total * weight / layer_outputs.shape[0]).astype(jnp.bfloat16)


def contract_rows(left, right):
    return lax.dot_general(
        left, right, (((0,), (0,)), ((), ())), preferred_element_type=jnp.float32
    )


def contract_cols(left, right):
    return lax.dot_general(
        left, right, (((1,), (1,)), ((), ())), preferred_element_type=jnp.float32
    )


def on_device(
    student_hidden, keep_index, lengths, teacher_layers, w_in, w_out, dec_in, dec_conv, dec_out
):
    copy_index = lax.axis_index("copy")
    units, keep_count, width = (
        student_hidden.shape[1],
        student_hidden.shape[2],
        student_hidden.shape[3],
    )
    frames = teacher_layers.shape[3]
    per_copy = teacher_layers.shape[2]
    layers = dec_conv.shape[1]
    kernel = dec_conv.shape[2]
    channels = dec_conv.shape[3]
    rows = units * keep_count
    masked_count = frames - keep_count
    frame_index = jnp.arange(frames, dtype=jnp.int32)
    valid = frame_index[None, :] < lengths[:, None]
    own_keep = lax.dynamic_index_in_dim(keep_index, copy_index, 0, keepdims=False)
    chosen = own_keep[:, None, :] == frame_index[None, :, None]
    own_kept = jnp.any(chosen, axis=2)
    select = chosen.astype(jnp.bfloat16)
    masked = jnp.logical_and(valid, jnp.logical_not(own_kept)).astype(jnp.float32)
    own_lengths = lax.dynamic_slice_in_dim(lengths, copy_index * per_copy, per_copy, 0)
    own_targets = teacher_targets(teacher_layers[:, 0], own_lengths)
    hidden_rows = student_hidden[0].reshape(rows, width).astype(jnp.float32)
    normed_exact, inv_scale = layer_norm(hidden_rows)
    normed = normed_exact.astype(jnp.bfloat16)
    w_in_all, w_out_all, dec_in_all, dec_conv_all, dec_out_all, targets = gather_all(
        w_in, w_out, dec_in, dec_conv, dec_out, own_targets
    )
    projected = jnp.dot(normed, w_in_all, preferred_element_type=jnp.float32)
    activation = gelu_value(projected).astype(jnp.bfloat16)
    mixed = jnp.dot(activation, w_out_all, preferred_element_type=jnp.float32)
    student_out = (hidden_rows + mixed).astype(jnp.bfloat16)
    lifted = jnp.dot(student_out, dec_in_all, preferred_element_type=jnp.float32).astype(
        jnp.bfloat16
    )
    state = jnp.einsum(
        "utk,ukc->utc",
        select,
        lifted.reshape(units, keep_count, channels),
        preferred_element_type=jnp.float32,
    ).astype(jnp.bfloat16)
    saved = []
    for layer in range(layers):
        unfolded = unfold_frames(state, kernel).reshape(units * frames, kernel * channels)
        convolved = jnp.dot(
            unfolded, dec_conv_all[layer], preferred_element_type=jnp.float32
        )
        conv_normed, conv_scale = layer_norm(convolved)
        result = gelu_value(conv_normed)
        if layer > 0:
            result = result + state.reshape(units * frames, channels).astype(jnp.float32)
        saved.append((unfolded, conv_normed, conv_scale))
        state = result.reshape(units, frames, channels).astype(jnp.bfloat16)
    final_state = state.reshape(units * frames, channels)
    prediction = jnp.dot(final_state, dec_out_all, preferred_element_type=jnp.float32)
    loss_scale = 1.0 / math.sqrt(width)
    error = (
        prediction - targets.reshape(units * frames, width).astype(jnp.float32)
    ) * masked.reshape(units * frames, 1)
    total = jnp.sum(error * error) * loss_scale
    prediction_grad = (2.0 * loss_scale * error).astype(jnp.bfloat16)
    out_term = contract_rows(final_state, prediction_grad)
    state_grad = contract_cols(prediction_grad, dec_out_all)
    kernel_terms = [None] * layers
    for layer in reversed(range(layers)):
        unfolded, conv_normed, conv_scale = saved[layer]
        filter_grad = norm_backward(
            state_grad * gelu_slope(conv_normed), conv_normed, conv_scale
        ).astype(jnp.bfloat16)
        kernel_terms[layer] = contract_rows(unfolded, filter_grad)
        unfold_grad = contract_cols(filter_grad, dec_conv_all[layer])
        previous_grad = fold_frames(
            unfold_grad.reshape(units, frames, kernel * channels), kernel, channels
        ).reshape(units * frames, channels)
        if layer > 0:
            previous_grad = previous_grad + state_grad
        state_grad = previous_grad
    conv_term = jnp.stack(
        [term.reshape(kernel, channels, channels).astype(jnp.bfloat16) for term in kernel_terms]
    )
    lifted_grad = (
        jnp.einsum(
            "utk,utc->ukc",
            select,
            state_grad.reshape(units, frames, channels).astype(jnp.bfloat16),
            preferred_element_type=jnp.float32,
        )
        .reshape(rows, channels)
        .astype(jnp.bfloat16)
    )
    in_term = contract_rows(student_out, lifted_grad)
    output_grad = contract_cols(lifted_grad, dec_in_all)
    output_half = output_grad.astype(jnp.bfloat16)
    activation_grad = contract_cols(output_half, w_out_all)
    projected_grad = (activation_grad * gelu_slope(projected)).astype(jnp.bfloat16)
    normed_grad = contract_cols(projected_grad, w_in_all)
    grad_hidden = (output_grad + norm_backward(normed_grad, normed_exact, inv_scale)).astype(
        jnp.bfloat16
    )
    *summed, loss_total = reduce_all(
        contract_rows(normed, projected_grad).astype(jnp.bfloat16),
        contract_rows(activation, output_half).astype(jnp.bfloat16),
        in_term.astype(jnp.bfloat16),
        conv_term,
        out_term.astype(jnp.bfloat16),
        jnp.full((8, 128), total, jnp.float32),
    )
    slot_total = lax.axis_size("copy") * lax.axis_size("fsdp") * units * masked_count
    loss = loss_total / float(slot_total)
    return (
        loss,
        grad_hidden.reshape(1, units, keep_count, width),
        *summed,
    )


def solution(mesh):
    placed = (
        P("copy", "fsdp", None, None),
        P(None, "fsdp", None),
        P("fsdp"),
        P(None, "copy", "fsdp", None, None),
        P("fsdp", None),
        P("fsdp", None),
        P("fsdp", None),
        P("fsdp", None, None, None),
        P("fsdp", None),
    )
    return jax.shard_map(
        on_device,
        mesh=mesh,
        in_specs=placed,
        out_specs=(
            P(),
            P("copy", "fsdp", None, None),
            P("fsdp", None),
            P("fsdp", None),
            P("fsdp", None),
            P("fsdp", None, None, None),
            P("fsdp", None),
        ),
        check_vma=False,
    )
```
